32 devices in a mesh: blk: 8 (over y, x, core), ma: 4 (over z).
Axes of the slice: x: 2, y: 2, z: 4, core: 2. Of those that a mesh axis runs over, the one named last changes fastest.
Arguments:
- sky_map: float32 [2, 256, 65536], P(None, ('blk', 'ma')), may hold values from -6 to 6
- legendre: bfloat16 [256, 64, 4096], P(('blk', 'ma')), as said below
- m_list: int32 [4, 16], replicated, may hold values from 0 to 32767, as said below
- block_start: int32 [64, 64], replicated, may hold values from 0 to 511, as said below
- beam_ratio: float32 [32768], replicated, may hold values from 0.5 to 2
Outputs:
- harmonics: float32 [2, 64, 4096], P(None, 'ma', 'blk')
- spectrum: float32 [4096], P('blk')
The draws below stay inside these ranges and needn't reach their ends.
Inputs may be any that keep to these rules, and one draw needn't show every extreme that they name: `m_list`: entries are distinct and equal one common offset plus multiples of 512. `block_start`: each row lists 64 distinct block numbers in increasing order. legendre[g, k, j] is zero wherever 64 * block_start[k, j // 64] + j mod 64 is below the k-th order of the flattened m_list.
All inputs are finite; a program needn't handle non-finite values.
Results may differ from the reference program's by a relative error of at most 0.0029.
Values may be sent and summed in bfloat16 or wider, within the bound.
A program may use at most 128 MiB of HBM per device.

```python
import math
import jax
import jax.numpy as jnp
from jax import lax

NPIX = 65536
LMAX = 32767
LBLK = 64
NB = 64
M_OWN = 16
M_WIN = 64
LW = 4096
CYCLES_N = 256


def window_lists(key):
    spacing = (LMAX + 1) // M_WIN
    offset_m = jax.random.randint(jax.random.fold_in(key, 11), (), 0, spacing)
    ordering = jax.random.permutation(jax.random.fold_in(key, 12), M_WIN)
    m_values = (offset_m + spacing * ordering).astype(jnp.int32)
    block_count = (LMAX + 1) // LBLK
    row_keys = jax.random.split(jax.random.fold_in(key, 13), M_WIN)

    def pick_blocks(row_key):
        return jnp.sort(jax.random.permutation(row_key, block_count)[:NB])
    blocks = jax.vmap(pick_blocks)(row_keys).astype(jnp.int32)
    return (m_values, blocks)


def draw_m_list(key, part):
    m_values, blocks = window_lists(key)
    return m_values.reshape(M_WIN // M_OWN, M_OWN)


def draw_block_start(key, part):
    m_values, blocks = window_lists(key)
    return blocks


def draw_legendre(key, part):
    m_values, blocks = window_lists(key)
    column = jnp.arange(LW, dtype=jnp.int32)
    degree = LBLK * blocks[:, column // LBLK] + column % LBLK
    live = (degree >= m_values[:, None]).astype(jnp.float32)
    value_key = jax.random.fold_in(key, 14)
    values = jax.random.normal(value_key, (CYCLES_N, M_WIN, LW), jnp.float32)
    return (values * live[None]).astype(jnp.bfloat16)


def shard_levels(stream_key, dims, cuts, low, largest):
    gain, own = 1.0, jax.random.fold_in(stream_key, 6)
    for dim, parts in cuts:
        draws = jnp.exp(jax.random.uniform(jax.random.fold_in(own, dim), (parts,), jnp.float32, low / len(cuts), largest / len(cuts)))
        gain = gain * jnp.repeat(draws, dims[dim] // parts).reshape([-1 if axis == dim else 1 for axis in range(len(dims))])
    return gain


def normal_values(own_key, extent, deviation, most, cuts=(), kind=jnp.bfloat16):
    level = shard_levels(own_key, extent, cuts, -0.22, 0.18) if cuts else 1.0
    drawn = jax.random.normal(own_key, extent, jnp.float32) * deviation * level
    return jnp.minimum(jnp.maximum(drawn, -most), most).astype(kind)


def setup_inputs(seed: int = 0) -> dict:
    key_of = jax.random.split(jax.random.key(seed), 6)
    sky_map = normal_values(key_of[0], (2, CYCLES_N, NPIX), 1.0, 6.0, ((1, 32),), jnp.float32)
    legendre = draw_legendre(jax.random.fold_in(key_of[5], 71), 0)
    m_list = draw_m_list(jax.random.fold_in(key_of[5], 71), 0)
    block_start = draw_block_start(jax.random.fold_in(key_of[5], 71), 0)
    beam_ratio = jnp.clip(jnp.exp(jax.random.uniform(key_of[4], (LMAX + 1,), jnp.float32, math.log(0.5), math.log(2.0))), 0.5, 2.0)
    return dict(sky_map=sky_map, legendre=legendre, m_list=m_list, block_start=block_start, beam_ratio=beam_ratio)


def cycle_fourier(sky, m_values, parity):
    hemispheres, cycle_rows, pixel_count = sky.shape
    flat_cycles = sky.reshape(hemispheres * cycle_rows, pixel_count)
    block_width = min(pixel_count, 8192)

    def add_block(running, block_index):
        segment = lax.dynamic_slice_in_dim(flat_cycles, block_index * block_width, block_width, 1)
        pixels = block_index * block_width + jnp.arange(block_width, dtype=jnp.int32)
        phase_turns = pixels[:, None] * m_values[None, :] % pixel_count
        angles = phase_turns.astype(jnp.float32) * (2.0 * math.pi / pixel_count)
        real_acc = running[0] + jnp.dot(segment, jnp.cos(angles), precision=lax.Precision.HIGHEST, preferred_element_type=jnp.float32)
        imag_acc = running[1] - jnp.dot(segment, jnp.sin(angles), precision=lax.Precision.HIGHEST, preferred_element_type=jnp.float32)
        return ((real_acc, imag_acc), block_index)
    empty_acc = jnp.zeros((hemispheres * cycle_rows, m_values.shape[0]), jnp.float32)
    sums, unused = lax.scan(add_block, (empty_acc, empty_acc), jnp.arange(pixel_count // block_width, dtype=jnp.int32))
    normalizer = 1.0 / math.sqrt(pixel_count)
    real_part = sums[0].reshape(hemispheres, cycle_rows, -1) * normalizer
    imag_part = sums[1].reshape(hemispheres, cycle_rows, -1) * normalizer
    twist = (parity[:, None] * m_values[None, :]).astype(jnp.float32) * (math.pi / pixel_count)
    cos_twist = jnp.cos(twist)
    sin_twist = jnp.sin(twist)
    rot_real = real_part * cos_twist + imag_part * sin_twist
    rot_imag = imag_part * cos_twist - real_part * sin_twist
    folded = jnp.stack([rot_real[0] + rot_real[1], rot_imag[0] + rot_imag[1], rot_real[0] - rot_real[1], rot_imag[0] - rot_imag[1]])
    return folded.astype(jnp.bfloat16)

def reference(sky_map, legendre, m_list, block_start, beam_ratio):
    m_values = m_list.reshape(-1)
    cycle_total = sky_map.shape[1]
    parity = jnp.arange(cycle_total, dtype=jnp.int32) % 2
    coeffs = cycle_fourier(sky_map, m_values, parity)
    factor_norm = 1.0 / math.sqrt(2.0 * cycle_total)
    column = jnp.arange(LW, dtype=jnp.int32)

    def one_order(order_index):
        leg_vals = lax.dynamic_index_in_dim(legendre, order_index, 1, keepdims=False)
        cycle_coeffs = lax.dynamic_index_in_dim(coeffs, order_index, 2, keepdims=False)
        products = jnp.dot(cycle_coeffs, leg_vals, preferred_element_type=jnp.float32)
        even_mask = (column + m_values[order_index]) % 2 == 0
        return jnp.where(even_mask[None, :], products[:2], products[2:]) * factor_norm
    partial_sum = lax.map(one_order, jnp.arange(M_WIN, dtype=jnp.int32))
    ratio_rows = beam_ratio.reshape(-1, LBLK)[block_start].reshape(M_WIN, LW)
    harmonics = jnp.transpose(partial_sum, (1, 0, 2)) * ratio_rows[None]
    spectrum = lax.optimization_barrier(jnp.sum(harmonics * harmonics, axis=(0, 1))) / M_WIN
    return (harmonics, spectrum)
```

```python
import functools
import math

import jax
import jax.numpy as jnp
from jax import lax
from jax.experimental import pallas as pl
from jax.experimental.pallas import tpu as pltpu
from jax.sharding import PartitionSpec as P

LBLK = 64
LANES = 128
MESH = pl.DeviceIdType.MESH


def cos_sin(steps, per_turn):
    quarter = per_turn // 4
    shift = quarter.bit_length() - 1
    quadrant = lax.shift_right_arithmetic(steps + quarter // 2, shift)
    y = (steps - quadrant * quarter).astype(jnp.float32) * (2.0 * math.pi / per_turn)
    z = y * y
    s = y * (1.0 + z * (-1.0 / 6 + z * (1.0 / 120 + z * (-1.0 / 5040 + z * (1.0 / 362880)))))
    c = 1.0 + z * (-0.5 + z * (1.0 / 24 + z * (-1.0 / 720 + z * (1.0 / 40320))))
    swap = (quadrant & 1) == 1
    cos = jnp.where(swap, s, c)
    sin = jnp.where(swap, c, s)
    cos = jnp.where(((quadrant + 1) & 2) == 2, -cos, cos)
    sin = jnp.where((quadrant & 2) == 2, -sin, sin)
    return cos, sin


def kernel(
    dims,
    sky_hbm,
    leg_hbm,
    m_ref,
    block_ref,
    beam_ref,
    harm_ref,
    spec_ref,
    sky,
    leg,
    fine,
    coarse,
    lhs,
    psend,
    own,
    precv,
    xsend,
    xrecv,
    plane_sum,
    zsend,
    zrecv,
    ratio,
    beam2,
    power,
    precv_power,
    sky_sem,
    leg_sem,
    psem,
    xsem,
    zsem,
    ssem,
):
    blk_n, ma_n, cycles, orders, own_n, degrees, npix, pieces = dims
    planes = blk_n // 2
    share = degrees // blk_n
    chunks = share // LANES
    period = 2 * orders
    q_all = npix // period
    q_fine = 16
    q_coarse = q_all // q_fine
    blk = lax.axis_index("blk")
    z = lax.axis_index("ma")
    core = blk % 2
    plane = blk // 2

    def flip(value, d):
        out, bit = 0, 1
        while bit <= d or bit == 1:
            digit = (value // bit) % 2
            out = out + bit * ((1 - digit) if d & bit else digit)
            bit *= 2
        return out + (value // bit) * bit

    sibling = (plane * 2 + 1 - core, z)
    plane_to = {d: flip(plane, d) for d in range(1, planes)}
    z_to = {d: flip(z, d) for d in range(1, ma_n)}

    width = npix // pieces
    sky_copies = [
        pltpu.make_async_copy(
            sky_hbm.at[:, :, pl.ds(i * width, width)],
            sky.at[:, :, pl.ds(i * width, width)],
            sky_sem.at[i],
        )
        for i in range(pieces)
    ]
    leg_copy = pltpu.make_async_copy(leg_hbm, leg, leg_sem)
    for copy in sky_copies:
        copy.start()
    leg_copy.start()

    barrier = pltpu.get_barrier_semaphore()
    partners = [sibling]
    partners += [(plane_to[d] * 2 + core, z) for d in range(1, planes)]
    partners += [(blk, z_to[d]) for d in range(1, ma_n)]
    for partner in partners:
        pl.semaphore_signal(barrier, inc=1, device_id=partner, device_id_type=MESH)

    m0 = m_ref[0, 0]
    lane = lax.broadcasted_iota(jnp.int32, (8, LANES), 1)
    m_vec = jnp.zeros((8, LANES), jnp.int32)
    for k in range(orders):
        m_vec = jnp.where(lane % orders == k, m_ref[k // own_n, k % own_n], m_vec)

    def fill(ref, count, step):
        index = lax.broadcasted_iota(jnp.int32, (count, 8, period), 0)
        c, s = cos_sin((index * (step * m0 % q_all)) % q_all, q_all)
        ref[0] = c
        ref[1] = s

    fill(fine, q_fine, 1)
    fill(coarse, q_coarse, q_fine)

    r_index = lax.broadcasted_iota(jnp.int32, (period, LANES), 0)
    tc, ts = cos_sin((r_index * m_vec[0:1]) % npix, npix)
    table = jnp.concatenate([tc, ts], axis=1)
    g_index = lax.broadcasted_iota(jnp.int32, (cycles, LANES), 0)
    first = (blk * ma_n + z) * cycles
    twist_c, twist_s = cos_sin(m_vec[0:1] * ((g_index + first) % 2), 2 * npix)

    zero = jnp.zeros((cycles, period), jnp.float32)

    def outer(i, acc):
        nc, ns, sc, ss = zero, zero, zero, zero
        for f in range(q_fine):
            at = pl.multiple_of((i * q_fine + f) * period, period)
            c, s = fine[0, f], fine[1, f]
            north = sky[0, :, pl.ds(at, period)]
            south = sky[1, :, pl.ds(at, period)]
            nc, ns = nc + north * c, ns + north * s
            sc, ss = sc + south * c, ss + south * s
        c, s = coarse[0, i], coarse[1, i]
        return (
            acc[0] + (nc * c - ns * s),
            acc[1] + (nc * s + ns * c),
            acc[2] + (sc * c - ss * s),
            acc[3] + (sc * s + ss * c),
        )

    acc = (zero, zero, zero, zero)
    per_piece = q_coarse // pieces
    for i in range(pieces):
        sky_copies[i].wait()
        acc = lax.fori_loop(i * per_piece, (i + 1) * per_piece, outer, acc)
    north_c, north_s, south_c, south_s = acc
    rows = jnp.concatenate(
        [north_c + south_c, north_c - south_c, north_s + south_s, north_s - south_s], axis=0
    )
    prod = jnp.dot(
        rows, table, precision=lax.Precision.HIGHEST, preferred_element_type=jnp.float32
    )
    scale = 1.0 / math.sqrt(npix)
    coeffs = []
    for h in range(2):
        by_c = prod[h * cycles : (h + 1) * cycles]
        by_s = prod[(2 + h) * cycles : (3 + h) * cycles]
        re = (by_c[:, :LANES] - by_s[:, LANES:]) * scale
        im = (by_c[:, LANES:] + by_s[:, :LANES]) * -scale
        coeffs.append(re * twist_c + im * twist_s)
        coeffs.append(im * twist_c - re * twist_s)

    dup = LANES // orders
    row = lax.broadcasted_iota(jnp.int32, (orders, LANES), 0)
    col = lax.broadcasted_iota(jnp.int32, (orders, LANES), 1)
    diagonal = row == col % orders
    for c in range(4):
        for p in range(cycles // dup):
            line = coeffs[c][p * dup : p * dup + 1]
            for e in range(1, dup):
                line = jnp.where(lane[0:1] >= e * orders, coeffs[c][p * dup + e : p * dup + e + 1], line)
            lhs[c * orders : (c + 1) * orders, p * LANES : (p + 1) * LANES] = jnp.where(
                diagonal, line, 0.0
            ).astype(jnp.bfloat16)

    even_lane = (lax.broadcasted_iota(jnp.int32, (2 * orders, 2 * LANES), 1) + m0) % 2 == 0
    leg_copy.wait()

    def contract(side, t, p):
        parts = []
        for e in range(2):
            at = pl.multiple_of((2 * (p + e) + side) * share + t * LANES, LANES)
            parts.append(leg[:, :, pl.ds(at, LANES)].reshape(cycles * orders, LANES))
        res = jnp.dot(
            lhs[...], jnp.concatenate(parts, axis=1), preferred_element_type=jnp.float32
        )
        return jnp.where(even_lane, res[: 2 * orders], res[2 * orders :])

    pcopies, xcopies, zcopies = {}, {}, {}

    def multiply(t):
        for p in range(0, planes, 2):
            res = contract(1 - core, t, p).astype(jnp.bfloat16)
            psend[t, p] = res[:, :LANES]
            psend[t, p + 1] = res[:, LANES:]
        if t == 0:
            pl.semaphore_wait(barrier, len(partners))
        pcopies[t] = pltpu.make_async_remote_copy(
            src_ref=psend.at[t],
            dst_ref=precv.at[t],
            send_sem=psem.at[0, t],
            recv_sem=psem.at[1, t],
            device_id=sibling,
            device_id_type=MESH,
        )
        pcopies[t].start()
        for p in range(0, planes, 2):
            res = contract(core, t, p)
            own[t, p] = res[:, :LANES]
            own[t, p + 1] = res[:, LANES:]

    def to_plane(t):
        pcopies[t].wait_recv()
        for d in range(planes - 1, 0, -1):
            other = plane_to[d]
            xsend[t, d - 1] = (own[t, other] + precv[t, other].astype(jnp.float32)).astype(
                jnp.bfloat16
            )
            copy = pltpu.make_async_remote_copy(
                src_ref=xsend.at[t, d - 1],
                dst_ref=xrecv.at[t, d - 1],
                send_sem=xsem.at[0, t, d - 1],
                recv_sem=xsem.at[1, t, d - 1],
                device_id=(other * 2 + core, z),
                device_id_type=MESH,
            )
            copy.start()
            xcopies[t, d] = copy

    def to_z(t):
        total = own[t, plane] + precv[t, plane].astype(jnp.float32)
        for d in range(1, planes):
            xcopies[t, d].wait_recv()
            total = total + xrecv[t, d - 1].astype(jnp.float32)
        plane_sum[t] = total.reshape(2, ma_n, own_n, LANES)
        for d in range(ma_n - 1, 0, -1):
            zsend[t, d - 1] = plane_sum[t, :, z_to[d]].astype(jnp.bfloat16)
            copy = pltpu.make_async_remote_copy(
                src_ref=zsend.at[t, d - 1],
                dst_ref=zrecv.at[t, d - 1],
                send_sem=zsem.at[0, t, d - 1],
                recv_sem=zsem.at[1, t, d - 1],
                device_id=(blk, z_to[d]),
                device_id_type=MESH,
            )
            copy.start()
            zcopies[t, d] = copy

    def beam_rows():
        rows_n = beam_ref.shape[0]
        beam2[:rows_n] = beam_ref[...]
        beam2[rows_n:] = pltpu.roll(beam_ref[...], LBLK, 1)
        low = lax.broadcasted_iota(jnp.int32, (1, LANES), 1) < LBLK

        def one(i, carry):
            for t in range(chunks):
                column = blk * (share // LBLK) + 2 * t
                b0 = block_ref[z * own_n + i, column]
                b1 = block_ref[z * own_n + i, column + 1]
                left = beam2[pl.ds((b0 % 2) * rows_n + b0 // 2, 1), :]
                right = beam2[pl.ds((1 - b1 % 2) * rows_n + b1 // 2, 1), :]
                ratio[t, pl.ds(i, 1), :] = jnp.where(low, left, right)
            return carry

        lax.fori_loop(0, own_n, one, 0)

    norm = 1.0 / math.sqrt(2.0 * cycles * blk_n * ma_n)

    def finish(t):
        total = plane_sum[t, :, z]
        for d in range(1, ma_n):
            zcopies[t, d].wait_recv()
            total = total + zrecv[t, d - 1].astype(jnp.float32)
        harm = total * norm * ratio[t][None]
        harm_ref[:, :, t * LANES : (t + 1) * LANES] = harm
        squares = jnp.sum(harm * harm, axis=(0, 1)) * (1.0 / orders)
        power[t : t + 1] = squares.reshape(1, LANES)

    for step in range(chunks + 3):
        if step < chunks:
            multiply(step)
        if 1 <= step <= chunks:
            to_plane(step - 1)
        if step == 2:
            beam_rows()
        if 2 <= step <= chunks + 1:
            to_z(step - 2)
        if 3 <= step:
            finish(step - 3)

    scopies = []
    for d in range(1, ma_n):
        copy = pltpu.make_async_remote_copy(
            src_ref=power,
            dst_ref=precv_power.at[d - 1],
            send_sem=ssem.at[0, d - 1],
            recv_sem=ssem.at[1, d - 1],
            device_id=(blk, z_to[d]),
            device_id_type=MESH,
        )
        copy.start()
        scopies.append(copy)
    for t in range(chunks):
        pcopies[t].wait_send()
        for d in range(1, planes):
            xcopies[t, d].wait_send()
        for d in range(1, ma_n):
            zcopies[t, d].wait_send()
    spectrum = power[...]
    for d in range(1, ma_n):
        scopies[d - 1].wait()
        spectrum = spectrum + precv_power[d - 1]
    for t in range(chunks):
        spec_ref[:, t * LANES : (t + 1) * LANES] = spectrum[t : t + 1]


def per_device(blk_n, ma_n, sky_map, legendre, m_list, block_start, beam_ratio):
    npix = sky_map.shape[2]
    cycles, orders, degrees = legendre.shape
    own_n = m_list.shape[1]
    share = degrees // blk_n
    chunks = share // LANES
    planes = blk_n // 2
    period = 2 * orders
    q_all = npix // period
    pieces = 4
    dims = (blk_n, ma_n, cycles, orders, own_n, degrees, npix, pieces)
    beam = beam_ratio.reshape(-1, LANES)
    f32, bf16 = jnp.float32, jnp.bfloat16
    dma = pltpu.SemaphoreType.DMA
    vmem = pl.BlockSpec(memory_space=pltpu.VMEM)
    smem = pl.BlockSpec(memory_space=pltpu.SMEM)
    anywhere = pl.BlockSpec(memory_space=pl.ANY)
    harm, spec = pl.pallas_call(
        functools.partial(kernel, dims),
        out_shape=(
            jax.ShapeDtypeStruct((2, own_n, share), f32),
            jax.ShapeDtypeStruct((1, share), f32),
        ),
        in_specs=[anywhere, anywhere, smem, smem, vmem],
        out_specs=(vmem, vmem),
        scratch_shapes=[
            pltpu.VMEM(sky_map.shape, f32),
            pltpu.VMEM(legendre.shape, bf16),
            pltpu.VMEM((2, 16, 8, period), f32),
            pltpu.VMEM((2, q_all // 16, 8, period), f32),
            pltpu.VMEM((4 * orders, cycles * orders), bf16),
            pltpu.VMEM((chunks, planes, 2 * orders, LANES), bf16),
            pltpu.VMEM((chunks, planes, 2 * orders, LANES), f32),
            pltpu.VMEM((chunks, planes, 2 * orders, LANES), bf16),
            pltpu.VMEM((chunks, planes - 1, 2 * orders, LANES), bf16),
            pltpu.VMEM((chunks, planes - 1, 2 * orders, LANES), bf16),
            pltpu.VMEM((chunks, 2, ma_n, own_n, LANES), f32),
            pltpu.VMEM((chunks, ma_n - 1, 2, own_n, LANES), bf16),
            pltpu.VMEM((chunks, ma_n - 1, 2, own_n, LANES), bf16),
            pltpu.VMEM((chunks, own_n, LANES), f32),
            pltpu.VMEM((2 * beam.shape[0], LANES), f32),
            pltpu.VMEM((chunks, LANES), f32),
            pltpu.VMEM((ma_n - 1, chunks, LANES), f32),
            dma((pieces,)),
            dma,
            dma((2, chunks)),
            dma((2, chunks, planes - 1)),
            dma((2, chunks, ma_n - 1)),
            dma((2, ma_n - 1)),
        ],
        compiler_params=pltpu.CompilerParams(
            collective_id=0, has_side_effects=True, vmem_limit_bytes=56 * 1024 * 1024
        ),
    )(sky_map, legendre, m_list, block_start, beam)
    return harm, spec.reshape(share)


def solution(mesh):
    placed = (P(None, ("blk", "ma"), None), P(("blk", "ma"), None, None), P(), P(), P())
    return jax.shard_map(
        functools.partial(per_device, mesh.shape["blk"], mesh.shape["ma"]),
        mesh=mesh,
        in_specs=placed,
        out_specs=(P(None, "ma", "blk"), P("blk")),
        check_vma=False,
    )
```

```python
import functools
import math

import jax
import jax.numpy as jnp
from jax import lax
from jax.experimental import pallas as pl
from jax.experimental.pallas import tpu as pltpu
from jax.sharding import PartitionSpec as P

LBLK = 64
CHUNKS = 2
LANES = 128
MESH = pl.DeviceIdType.MESH


def cos_sin(steps, per_turn):
    quarter = per_turn // 4
    shift = quarter.bit_length() - 1
    quadrant = lax.shift_right_arithmetic(steps + quarter // 2, shift)
    y = (steps - quadrant * quarter).astype(jnp.float32) * (2.0 * math.pi / per_turn)
    z = y * y
    s = y * (1.0 + z * (-1.0 / 6 + z * (1.0 / 120 + z * (-1.0 / 5040 + z * (1.0 / 362880)))))
    c = 1.0 + z * (-0.5 + z * (1.0 / 24 + z * (-1.0 / 720 + z * (1.0 / 40320))))
    swap = (quadrant & 1) == 1
    cos = jnp.where(swap, s, c)
    sin = jnp.where(swap, c, s)
    cos = jnp.where(((quadrant + 1) & 2) == 2, -cos, cos)
    sin = jnp.where((quadrant & 2) == 2, -sin, sin)
    return cos, sin


def kernel(
    dims,
    sky_hbm,
    leg_hbm,
    m_hbm,
    block_hbm,
    beam_hbm,
    harm_ref,
    spec_ref,
    m_ref,
    block_ref,
    beam_ref,
    sky,
    leg,
    fine,
    coarse,
    lhs,
    psend,
    own,
    precv,
    xsend,
    xrecv,
    plane_sum,
    zsend,
    zrecv,
    ratio,
    beam2,
    power,
    precv_power,
    small_sem,
    sky_sem,
    leg_sem,
    psem,
    xsem,
    zsem,
    ssem,
):
    blk_n, ma_n, cycles, orders, own_n, degrees, npix, pieces, chunks = dims
    planes = blk_n // 2
    share = degrees // blk_n
    wide = share // chunks
    period = 2 * orders
    q_all = npix // period
    q_fine = 16
    q_coarse = q_all // q_fine
    blk = lax.axis_index("blk")
    z = lax.axis_index("ma")
    core = blk % 2
    plane = blk // 2

    def flip(value, d):
        out, bit = 0, 1
        while bit <= d or bit == 1:
            digit = (value // bit) % 2
            out = out + bit * ((1 - digit) if d & bit else digit)
            bit *= 2
        return out + (value // bit) * bit

    sibling = (plane * 2 + 1 - core, z)
    plane_to = {d: flip(plane, d) for d in range(1, planes)}
    z_to = {d: flip(z, d) for d in range(1, ma_n)}

    width = npix // pieces
    sky_copies = [
        pltpu.make_async_copy(
            sky_hbm.at[:, :, pl.ds(i * width, width)],
            sky.at[:, :, pl.ds(i * width, width)],
            sky_sem.at[i],
        )
        for i in range(pieces)
    ]
    leg_copy = pltpu.make_async_copy(leg_hbm, leg, leg_sem)
    m_copy = pltpu.make_async_copy(m_hbm, m_ref, small_sem.at[0])
    block_copy = pltpu.make_async_copy(block_hbm, block_ref, small_sem.at[1])
    beam_copy = pltpu.make_async_copy(beam_hbm, beam_ref, small_sem.at[2])
    m_copy.start()
    block_copy.start()
    beam_copy.start()
    for copy in sky_copies:
        copy.start()
    leg_copy.start()

    barrier = pltpu.get_barrier_semaphore()
    partners = [sibling]
    partners += [(plane_to[d] * 2 + core, z) for d in range(1, planes)]
    partners += [(blk, z_to[d]) for d in range(1, ma_n)]
    for partner in partners:
        pl.semaphore_signal(barrier, inc=1, device_id=partner, device_id_type=MESH)

    m_copy.wait()
    m0 = m_ref[0, 0]
    lane = lax.broadcasted_iota(jnp.int32, (8, LANES), 1)
    m_vec = jnp.zeros((8, LANES), jnp.int32)
    for k in range(orders):
        m_vec = jnp.where(lane % orders == k, m_ref[k // own_n, k % own_n], m_vec)

    def fill(ref, count, step):
        index = lax.broadcasted_iota(jnp.int32, (count, 8, period), 0)
        c, s = cos_sin((index * (step * m0 % q_all)) % q_all, q_all)
        ref[0] = c
        ref[1] = s

    fill(fine, q_fine, 1)
    fill(coarse, q_coarse, q_fine)

    r_index = lax.broadcasted_iota(jnp.int32, (period, LANES), 0)
    tc, ts = cos_sin((r_index * m_vec[0:1]) % npix, npix)
    table = jnp.concatenate([tc, ts], axis=1)
    g_index = lax.broadcasted_iota(jnp.int32, (cycles, LANES), 0)
    first = (blk * ma_n + z) * cycles
    twist_c, twist_s = cos_sin(m_vec[0:1] * ((g_index + first) % 2), 2 * npix)

    def beam_rows():
        rows_n = beam_ref.shape[0]
        beam2[:rows_n] = beam_ref[...]
        beam2[rows_n:] = pltpu.roll(beam_ref[...], LBLK, 1)
        low = lax.broadcasted_iota(jnp.int32, (1, LANES), 1) < LBLK

        def one(i, carry):
            for t in range(share // LANES):
                column = blk * (share // LBLK) + 2 * t
                b0 = block_ref[z * own_n + i, column]
                b1 = block_ref[z * own_n + i, column + 1]
                left = beam2[pl.ds((b0 % 2) * rows_n + b0 // 2, 1), :]
                right = beam2[pl.ds((1 - b1 % 2) * rows_n + b1 // 2, 1), :]
                ratio[t, pl.ds(i, 1), :] = jnp.where(low, left, right)
            return carry

        lax.fori_loop(0, own_n, one, 0)

    block_copy.wait()
    beam_copy.wait()
    beam_rows()

    zero = jnp.zeros((cycles, period), jnp.float32)

    def outer(i, acc):
        nc, ns, sc, ss = zero, zero, zero, zero
        for f in range(q_fine):
            at = pl.multiple_of((i * q_fine + f) * period, period)
            c, s = fine[0, f], fine[1, f]
            north = sky[0, :, pl.ds(at, period)]
            south = sky[1, :, pl.ds(at, period)]
            nc, ns = nc + north * c, ns + north * s
            sc, ss = sc + south * c, ss + south * s
        c, s = coarse[0, i], coarse[1, i]
        return (
            acc[0] + (nc * c - ns * s),
            acc[1] + (nc * s + ns * c),
            acc[2] + (sc * c - ss * s),
            acc[3] + (sc * s + ss * c),
        )

    acc = (zero, zero, zero, zero)
    per_piece = q_coarse // pieces
    for i in range(pieces):
        sky_copies[i].wait()
        acc = lax.fori_loop(i * per_piece, (i + 1) * per_piece, outer, acc)
    north_c, north_s, south_c, south_s = acc
    rows = jnp.concatenate(
        [north_c + south_c, north_c - south_c, north_s + south_s, north_s - south_s], axis=0
    )
    prod = jnp.dot(
        rows, table, precision=lax.Precision.HIGHEST, preferred_element_type=jnp.float32
    )
    scale = 1.0 / math.sqrt(npix)
    coeffs = []
    for h in range(2):
        by_c = prod[h * cycles : (h + 1) * cycles]
        by_s = prod[(2 + h) * cycles : (3 + h) * cycles]
        re = (by_c[:, :LANES] - by_s[:, LANES:]) * scale
        im = (by_c[:, LANES:] + by_s[:, :LANES]) * -scale
        coeffs.append(re * twist_c + im * twist_s)
        coeffs.append(im * twist_c - re * twist_s)

    dup = LANES // orders
    row = lax.broadcasted_iota(jnp.int32, (orders, LANES), 0)
    col = lax.broadcasted_iota(jnp.int32, (orders, LANES), 1)
    diagonal = row == col % orders
    for c in range(4):
        for p in range(cycles // dup):
            line = coeffs[c][p * dup : p * dup + 1]
            for e in range(1, dup):
                line = jnp.where(lane[0:1] >= e * orders, coeffs[c][p * dup + e : p * dup + e + 1], line)
            lhs[c * orders : (c + 1) * orders, p * LANES : (p + 1) * LANES] = jnp.where(
                diagonal, line, 0.0
            ).astype(jnp.bfloat16)

    group = max(1, 2 * LANES // wide)
    even_lane = (lax.broadcasted_iota(jnp.int32, (2 * orders, group * wide), 1) + m0) % 2 == 0
    leg_copy.wait()

    def contract(side, t, p):
        parts = []
        for e in range(group):
            at = pl.multiple_of((2 * (p + e) + side) * share + t * wide, LANES)
            parts.append(leg[:, :, pl.ds(at, wide)].reshape(cycles * orders, wide))
        right = parts[0] if group == 1 else jnp.concatenate(parts, axis=1)
        res = jnp.dot(lhs[...], right, preferred_element_type=jnp.float32)
        return jnp.where(even_lane, res[: 2 * orders], res[2 * orders :])

    pcopies, xcopies, zcopies = {}, {}, {}

    def multiply(t):
        for p in range(0, planes, group):
            res = contract(1 - core, t, p).astype(jnp.bfloat16)
            for e in range(group):
                psend[t, p + e] = res[:, e * wide : (e + 1) * wide]
        if t == 0:
            pl.semaphore_wait(barrier, len(partners))
        pcopies[t] = pltpu.make_async_remote_copy(
            src_ref=psend.at[t],
            dst_ref=precv.at[t],
            send_sem=psem.at[0, t],
            recv_sem=psem.at[1, t],
            device_id=sibling,
            device_id_type=MESH,
        )
        pcopies[t].start()
        for p in range(0, planes, group):
            res = contract(core, t, p)
            for e in range(group):
                own[t, p + e] = res[:, e * wide : (e + 1) * wide]

    def to_plane(t):
        pcopies[t].wait_recv()
        for d in range(planes - 1, 0, -1):
            other = plane_to[d]
            xsend[t, d - 1] = (own[t, other] + precv[t, other].astype(jnp.float32)).astype(
                jnp.bfloat16
            )
            copy = pltpu.make_async_remote_copy(
                src_ref=xsend.at[t, d - 1],
                dst_ref=xrecv.at[t, d - 1],
                send_sem=xsem.at[0, t, d - 1],
                recv_sem=xsem.at[1, t, d - 1],
                device_id=(other * 2 + core, z),
                device_id_type=MESH,
            )
            copy.start()
            xcopies[t, d] = copy

    def to_z(t):
        total = own[t, plane] + precv[t, plane].astype(jnp.float32)
        for d in range(1, planes):
            xcopies[t, d].wait_recv()
            total = total + xrecv[t, d - 1].astype(jnp.float32)
        plane_sum[t] = total.reshape(2, ma_n, own_n, wide)
        for d in range(ma_n - 1, 0, -1):
            zsend[t, d - 1] = plane_sum[t, :, z_to[d]].astype(jnp.bfloat16)
            copy = pltpu.make_async_remote_copy(
                src_ref=zsend.at[t, d - 1],
                dst_ref=zrecv.at[t, d - 1],
                send_sem=zsem.at[0, t, d - 1],
                recv_sem=zsem.at[1, t, d - 1],
                device_id=(blk, z_to[d]),
                device_id_type=MESH,
            )
            copy.start()
            zcopies[t, d] = copy

    norm = 1.0 / math.sqrt(2.0 * cycles * blk_n * ma_n)

    def finish(t):
        total = plane_sum[t, :, z]
        for d in range(1, ma_n):
            zcopies[t, d].wait_recv()
            total = total + zrecv[t, d - 1].astype(jnp.float32)
        tiles = wide // LANES
        beam_rows_t = jnp.concatenate([ratio[t * tiles + i] for i in range(tiles)], axis=1)
        harm = total * norm * beam_rows_t[None]
        harm_ref[:, :, t * wide : (t + 1) * wide] = harm
        squares = jnp.sum(harm * harm, axis=(0, 1)) * (1.0 / orders)
        power[:, t * wide : (t + 1) * wide] = squares.reshape(1, wide)

    for step in range(chunks + 3):
        if step < chunks:
            multiply(step)
        if 1 <= step <= chunks:
            to_plane(step - 1)
        if 2 <= step <= chunks + 1:
            to_z(step - 2)
        if 3 <= step:
            finish(step - 3)

    scopies = []
    for d in range(1, ma_n):
        copy = pltpu.make_async_remote_copy(
            src_ref=power,
            dst_ref=precv_power.at[d - 1],
            send_sem=ssem.at[0, d - 1],
            recv_sem=ssem.at[1, d - 1],
            device_id=(blk, z_to[d]),
            device_id_type=MESH,
        )
        copy.start()
        scopies.append(copy)
    for t in range(chunks):
        pcopies[t].wait_send()
        for d in range(1, planes):
            xcopies[t, d].wait_send()
        for d in range(1, ma_n):
            zcopies[t, d].wait_send()
    spectrum = power[...]
    for d in range(1, ma_n):
        scopies[d - 1].wait()
        spectrum = spectrum + precv_power[d - 1]
    spec_ref[...] = spectrum


def hand_on(harm_in, spec_in, harm_out, spec_out):
    harm_out[...] = harm_in[...]
    spec_out[...] = spec_in[...]


def per_device(blk_n, ma_n, sky_map, legendre, m_list, block_start, beam_ratio):
    npix = sky_map.shape[2]
    cycles, orders, degrees = legendre.shape
    own_n = m_list.shape[1]
    share = degrees // blk_n
    chunks = CHUNKS
    wide = share // chunks
    planes = blk_n // 2
    period = 2 * orders
    q_all = npix // period
    pieces = 4
    dims = (blk_n, ma_n, cycles, orders, own_n, degrees, npix, pieces, chunks)
    beam = beam_ratio.reshape(-1, LANES)
    f32, bf16 = jnp.float32, jnp.bfloat16
    dma = pltpu.SemaphoreType.DMA
    vmem = pl.BlockSpec(memory_space=pltpu.VMEM)
    anywhere = pl.BlockSpec(memory_space=pl.ANY)
    harm, spec = pl.pallas_call(
        functools.partial(kernel, dims),
        out_shape=(
            jax.ShapeDtypeStruct((2, own_n, share), f32),
            jax.ShapeDtypeStruct((1, share), f32),
        ),
        in_specs=[anywhere] * 5,
        out_specs=(vmem, vmem),
        scratch_shapes=[
            pltpu.SMEM(m_list.shape, jnp.int32),
            pltpu.SMEM(block_start.shape, jnp.int32),
            pltpu.VMEM(beam.shape, f32),
            pltpu.VMEM(sky_map.shape, f32),
            pltpu.VMEM(legendre.shape, bf16),
            pltpu.VMEM((2, 16, 8, period), f32),
            pltpu.VMEM((2, q_all // 16, 8, period), f32),
            pltpu.VMEM((4 * orders, cycles * orders), bf16),
            pltpu.VMEM((chunks, planes, 2 * orders, wide), bf16),
            pltpu.VMEM((chunks, planes, 2 * orders, wide), f32),
            pltpu.VMEM((chunks, planes, 2 * orders, wide), bf16),
            pltpu.VMEM((chunks, planes - 1, 2 * orders, wide), bf16),
            pltpu.VMEM((chunks, planes - 1, 2 * orders, wide), bf16),
            pltpu.VMEM((chunks, 2, ma_n, own_n, wide), f32),
            pltpu.VMEM((chunks, ma_n - 1, 2, own_n, wide), bf16),
            pltpu.VMEM((chunks, ma_n - 1, 2, own_n, wide), bf16),
            pltpu.VMEM((share // LANES, own_n, LANES), f32),
            pltpu.VMEM((2 * beam.shape[0], LANES), f32),
            pltpu.VMEM((1, share), f32),
            pltpu.VMEM((ma_n - 1, 1, share), f32),
            dma((3,)),
            dma((pieces,)),
            dma,
            dma((2, chunks)),
            dma((2, chunks, planes - 1)),
            dma((2, chunks, ma_n - 1)),
            dma((2, ma_n - 1)),
        ],
        compiler_params=pltpu.CompilerParams(
            collective_id=0, has_side_effects=True, vmem_limit_bytes=56 * 1024 * 1024
        ),
    )(sky_map, legendre, m_list, block_start, beam)
    harm, spec = pl.pallas_call(
        hand_on,
        out_shape=(jax.ShapeDtypeStruct(harm.shape, f32), jax.ShapeDtypeStruct(spec.shape, f32)),
        in_specs=[vmem] * 2,
        out_specs=(vmem, vmem),
    )(harm, spec)
    return harm, spec.reshape(share)


def solution(mesh):
    placed = (P(None, ("blk", "ma"), None), P(("blk", "ma"), None, None), P(), P(), P())
    return jax.shard_map(
        functools.partial(per_device, mesh.shape["blk"], mesh.shape["ma"]),
        mesh=mesh,
        in_specs=placed,
        out_specs=(P(None, "ma", "blk"), P("blk")),
        check_vma=False,
    )
```

```python
import functools
import math

import jax
import jax.numpy as jnp
from jax import lax
from jax.experimental import pallas as pl
from jax.experimental.pallas import tpu as pltpu
from jax.sharding import PartitionSpec as P

LBLK = 64
CHUNKS = 2
LANES = 128
MESH = pl.DeviceIdType.MESH


def cos_sin(steps, per_turn):
    quarter = per_turn // 4
    shift = quarter.bit_length() - 1
    quadrant = lax.shift_right_arithmetic(steps + quarter // 2, shift)
    y = (steps - quadrant * quarter).astype(jnp.float32) * (2.0 * math.pi / per_turn)
    z = y * y
    s = y * (1.0 + z * (-1.0 / 6 + z * (1.0 / 120 + z * (-1.0 / 5040 + z * (1.0 / 362880)))))
    c = 1.0 + z * (-0.5 + z * (1.0 / 24 + z * (-1.0 / 720 + z * (1.0 / 40320))))
    swap = (quadrant & 1) == 1
    cos = jnp.where(swap, s, c)
    sin = jnp.where(swap, c, s)
    cos = jnp.where(((quadrant + 1) & 2) == 2, -cos, cos)
    sin = jnp.where((quadrant & 2) == 2, -sin, sin)
    return cos, sin


def kernel(
    dims,
    sky_hbm,
    leg_hbm,
    m_hbm,
    block_hbm,
    beam_hbm,
    harm_ref,
    spec_ref,
    harm_vmem,
    m_ref,
    block_ref,
    beam_ref,
    sky,
    leg,
    fine,
    coarse,
    lhs,
    psend,
    own,
    precv,
    xsend,
    xrecv,
    plane_sum,
    zsend,
    zrecv,
    ratio,
    beam2,
    power,
    precv_power,
    small_sem,
    out_sem,
    sky_sem,
    leg_sem,
    psem,
    xsem,
    zsem,
    ssem,
):
    blk_n, ma_n, cycles, orders, own_n, degrees, npix, pieces, chunks = dims
    planes = blk_n // 2
    share = degrees // blk_n
    wide = share // chunks
    period = 2 * orders
    q_all = npix // period
    q_fine = 16
    q_coarse = q_all // q_fine
    blk = lax.axis_index("blk")
    z = lax.axis_index("ma")
    core = blk % 2
    plane = blk // 2

    def flip(value, d):
        out, bit = 0, 1
        while bit <= d or bit == 1:
            digit = (value // bit) % 2
            out = out + bit * ((1 - digit) if d & bit else digit)
            bit *= 2
        return out + (value // bit) * bit

    sibling = (plane * 2 + 1 - core, z)
    plane_to = {d: flip(plane, d) for d in range(1, planes)}
    z_to = {d: flip(z, d) for d in range(1, ma_n)}

    width = npix // pieces
    sky_copies = [
        pltpu.make_async_copy(
            sky_hbm.at[:, :, pl.ds(i * width, width)],
            sky.at[:, :, pl.ds(i * width, width)],
            sky_sem.at[i],
        )
        for i in range(pieces)
    ]
    leg_copy = pltpu.make_async_copy(leg_hbm, leg, leg_sem)
    m_copy = pltpu.make_async_copy(m_hbm, m_ref, small_sem.at[0])
    block_copy = pltpu.make_async_copy(block_hbm, block_ref, small_sem.at[1])
    beam_copy = pltpu.make_async_copy(beam_hbm, beam_ref, small_sem.at[2])
    m_copy.start()
    block_copy.start()
    beam_copy.start()
    for copy in sky_copies:
        copy.start()
    leg_copy.start()

    barrier = pltpu.get_barrier_semaphore()
    partners = [sibling]
    partners += [(plane_to[d] * 2 + core, z) for d in range(1, planes)]
    partners += [(blk, z_to[d]) for d in range(1, ma_n)]
    for partner in partners:
        pl.semaphore_signal(barrier, inc=1, device_id=partner, device_id_type=MESH)

    m_copy.wait()
    m0 = m_ref[0, 0]
    lane = lax.broadcasted_iota(jnp.int32, (8, LANES), 1)
    m_vec = jnp.zeros((8, LANES), jnp.int32)
    for k in range(orders):
        m_vec = jnp.where(lane % orders == k, m_ref[k // own_n, k % own_n], m_vec)

    def fill(ref, count, step):
        index = lax.broadcasted_iota(jnp.int32, (count, 8, period), 0)
        c, s = cos_sin((index * (step * m0 % q_all)) % q_all, q_all)
        ref[0] = c
        ref[1] = s

    fill(fine, q_fine, 1)
    fill(coarse, q_coarse, q_fine)

    r_index = lax.broadcasted_iota(jnp.int32, (period, LANES), 0)
    tc, ts = cos_sin((r_index * m_vec[0:1]) % npix, npix)
    table = jnp.concatenate([tc, ts], axis=1)
    g_index = lax.broadcasted_iota(jnp.int32, (cycles, LANES), 0)
    first = (blk * ma_n + z) * cycles
    twist_c, twist_s = cos_sin(m_vec[0:1] * ((g_index + first) % 2), 2 * npix)

    def beam_rows():
        rows_n = beam_ref.shape[0]
        beam2[:rows_n] = beam_ref[...]
        beam2[rows_n:] = pltpu.roll(beam_ref[...], LBLK, 1)
        low = lax.broadcasted_iota(jnp.int32, (1, LANES), 1) < LBLK

        def one(i, carry):
            for t in range(share // LANES):
                column = blk * (share // LBLK) + 2 * t
                b0 = block_ref[z * own_n + i, column]
                b1 = block_ref[z * own_n + i, column + 1]
                left = beam2[pl.ds((b0 % 2) * rows_n + b0 // 2, 1), :]
                right = beam2[pl.ds((1 - b1 % 2) * rows_n + b1 // 2, 1), :]
                ratio[t, pl.ds(i, 1), :] = jnp.where(low, left, right)
            return carry

        lax.fori_loop(0, own_n, one, 0)

    zero = jnp.zeros((cycles, period), jnp.float32)

    def outer(i, acc):
        nc, ns, sc, ss = zero, zero, zero, zero
        for f in range(q_fine):
            at = pl.multiple_of((i * q_fine + f) * period, period)
            c, s = fine[0, f], fine[1, f]
            north = sky[0, :, pl.ds(at, period)]
            south = sky[1, :, pl.ds(at, period)]
            nc, ns = nc + north * c, ns + north * s
            sc, ss = sc + south * c, ss + south * s
        c, s = coarse[0, i], coarse[1, i]
        return (
            acc[0] + (nc * c - ns * s),
            acc[1] + (nc * s + ns * c),
            acc[2] + (sc * c - ss * s),
            acc[3] + (sc * s + ss * c),
        )

    acc = (zero, zero, zero, zero)
    per_piece = q_coarse // pieces
    for i in range(pieces):
        sky_copies[i].wait()
        acc = lax.fori_loop(i * per_piece, (i + 1) * per_piece, outer, acc)
    north_c, north_s, south_c, south_s = acc
    rows = jnp.concatenate(
        [north_c + south_c, north_c - south_c, north_s + south_s, north_s - south_s], axis=0
    )
    prod = jnp.dot(
        rows, table, precision=lax.Precision.HIGHEST, preferred_element_type=jnp.float32
    )
    scale = 1.0 / math.sqrt(npix)
    coeffs = []
    for h in range(2):
        by_c = prod[h * cycles : (h + 1) * cycles]
        by_s = prod[(2 + h) * cycles : (3 + h) * cycles]
        re = (by_c[:, :LANES] - by_s[:, LANES:]) * scale
        im = (by_c[:, LANES:] + by_s[:, :LANES]) * -scale
        coeffs.append(re * twist_c + im * twist_s)
        coeffs.append(im * twist_c - re * twist_s)

    dup = LANES // orders
    row = lax.broadcasted_iota(jnp.int32, (orders, LANES), 0)
    col = lax.broadcasted_iota(jnp.int32, (orders, LANES), 1)
    diagonal = row == col % orders
    for c in range(4):
        for p in range(cycles // dup):
            line = coeffs[c][p * dup : p * dup + 1]
            for e in range(1, dup):
                line = jnp.where(lane[0:1] >= e * orders, coeffs[c][p * dup + e : p * dup + e + 1], line)
            lhs[c * orders : (c + 1) * orders, p * LANES : (p + 1) * LANES] = jnp.where(
                diagonal, line, 0.0
            ).astype(jnp.bfloat16)

    group = max(1, 2 * LANES // wide)
    even_lane = (lax.broadcasted_iota(jnp.int32, (2 * orders, group * wide), 1) + m0) % 2 == 0
    leg_copy.wait()

    def contract(side, t, p):
        parts = []
        for e in range(group):
            at = pl.multiple_of((2 * (p + e) + side) * share + t * wide, LANES)
            parts.append(leg[:, :, pl.ds(at, wide)].reshape(cycles * orders, wide))
        right = parts[0] if group == 1 else jnp.concatenate(parts, axis=1)
        res = jnp.dot(lhs[...], right, preferred_element_type=jnp.float32)
        return jnp.where(even_lane, res[: 2 * orders], res[2 * orders :])

    pcopies, xcopies, zcopies = {}, {}, {}

    def multiply(t):
        for p in range(0, planes, group):
            res = contract(1 - core, t, p).astype(jnp.bfloat16)
            for e in range(group):
                psend[t, p + e] = res[:, e * wide : (e + 1) * wide]
        if t == 0:
            pl.semaphore_wait(barrier, len(partners))
        pcopies[t] = pltpu.make_async_remote_copy(
            src_ref=psend.at[t],
            dst_ref=precv.at[t],
            send_sem=psem.at[0, t],
            recv_sem=psem.at[1, t],
            device_id=sibling,
            device_id_type=MESH,
        )
        pcopies[t].start()
        for p in range(0, planes, group):
            res = contract(core, t, p)
            for e in range(group):
                own[t, p + e] = res[:, e * wide : (e + 1) * wide]

    def to_plane(t):
        pcopies[t].wait_recv()
        for d in range(planes - 1, 0, -1):
            other = plane_to[d]
            xsend[t, d - 1] = (own[t, other] + precv[t, other].astype(jnp.float32)).astype(
                jnp.bfloat16
            )
            copy = pltpu.make_async_remote_copy(
                src_ref=xsend.at[t, d - 1],
                dst_ref=xrecv.at[t, d - 1],
                send_sem=xsem.at[0, t, d - 1],
                recv_sem=xsem.at[1, t, d - 1],
                device_id=(other * 2 + core, z),
                device_id_type=MESH,
            )
            copy.start()
            xcopies[t, d] = copy

    def to_z(t):
        total = own[t, plane] + precv[t, plane].astype(jnp.float32)
        for d in range(1, planes):
            xcopies[t, d].wait_recv()
            total = total + xrecv[t, d - 1].astype(jnp.float32)
        plane_sum[t] = total.reshape(2, ma_n, own_n, wide)
        for d in range(ma_n - 1, 0, -1):
            zsend[t, d - 1] = plane_sum[t, :, z_to[d]].astype(jnp.bfloat16)
            copy = pltpu.make_async_remote_copy(
                src_ref=zsend.at[t, d - 1],
                dst_ref=zrecv.at[t, d - 1],
                send_sem=zsem.at[0, t, d - 1],
                recv_sem=zsem.at[1, t, d - 1],
                device_id=(blk, z_to[d]),
                device_id_type=MESH,
            )
            copy.start()
            zcopies[t, d] = copy

    norm = 1.0 / math.sqrt(2.0 * cycles * blk_n * ma_n)

    def finish(t):
        total = plane_sum[t, :, z]
        for d in range(1, ma_n):
            zcopies[t, d].wait_recv()
            total = total + zrecv[t, d - 1].astype(jnp.float32)
        tiles = wide // LANES
        beam_rows_t = jnp.concatenate([ratio[t * tiles + i] for i in range(tiles)], axis=1)
        harm = total * norm * beam_rows_t[None]
        harm_vmem[:, :, t * wide : (t + 1) * wide] = harm
        squares = jnp.sum(harm * harm, axis=(0, 1)) * (1.0 / orders)
        power[:, t * wide : (t + 1) * wide] = squares.reshape(1, wide)

    for step in range(chunks + 3):
        if step < chunks:
            multiply(step)
        if 1 <= step <= chunks:
            to_plane(step - 1)
        if step == 2:
            block_copy.wait()
            beam_copy.wait()
            beam_rows()
        if 2 <= step <= chunks + 1:
            to_z(step - 2)
        if 3 <= step:
            finish(step - 3)

    scopies = []
    for d in range(1, ma_n):
        copy = pltpu.make_async_remote_copy(
            src_ref=power,
            dst_ref=precv_power.at[d - 1],
            send_sem=ssem.at[0, d - 1],
            recv_sem=ssem.at[1, d - 1],
            device_id=(blk, z_to[d]),
            device_id_type=MESH,
        )
        copy.start()
        scopies.append(copy)
    out_copy = pltpu.make_async_copy(harm_vmem, harm_ref, out_sem)
    out_copy.start()
    for t in range(chunks):
        pcopies[t].wait_send()
        for d in range(1, planes):
            xcopies[t, d].wait_send()
        for d in range(1, ma_n):
            zcopies[t, d].wait_send()
    spectrum = power[...]
    for d in range(1, ma_n):
        scopies[d - 1].wait()
        spectrum = spectrum + precv_power[d - 1]
    spec_ref[...] = spectrum
    out_copy.wait()


def hand_on(harm_in, spec_in, harm_out, spec_out):
    harm_out[...] = harm_in[...]
    spec_out[...] = spec_in[...]


def per_device(blk_n, ma_n, sky_map, legendre, m_list, block_start, beam_ratio):
    npix = sky_map.shape[2]
    cycles, orders, degrees = legendre.shape
    own_n = m_list.shape[1]
    share = degrees // blk_n
    chunks = CHUNKS
    wide = share // chunks
    planes = blk_n // 2
    period = 2 * orders
    q_all = npix // period
    pieces = 4
    dims = (blk_n, ma_n, cycles, orders, own_n, degrees, npix, pieces, chunks)
    beam = beam_ratio.reshape(-1, LANES)
    f32, bf16 = jnp.float32, jnp.bfloat16
    dma = pltpu.SemaphoreType.DMA
    vmem = pl.BlockSpec(memory_space=pltpu.VMEM)
    anywhere = pl.BlockSpec(memory_space=pl.ANY)
    harm, spec = pl.pallas_call(
        functools.partial(kernel, dims),
        out_shape=(
            jax.ShapeDtypeStruct((2, own_n, share), f32),
            jax.ShapeDtypeStruct((1, share), f32),
        ),
        in_specs=[anywhere] * 5,
        out_specs=(anywhere, vmem),
        scratch_shapes=[
            pltpu.VMEM((2, own_n, share), f32),
            pltpu.SMEM(m_list.shape, jnp.int32),
            pltpu.SMEM(block_start.shape, jnp.int32),
            pltpu.VMEM(beam.shape, f32),
            pltpu.VMEM(sky_map.shape, f32),
            pltpu.VMEM(legendre.shape, bf16),
            pltpu.VMEM((2, 16, 8, period), f32),
            pltpu.VMEM((2, q_all // 16, 8, period), f32),
            pltpu.VMEM((4 * orders, cycles * orders), bf16),
            pltpu.VMEM((chunks, planes, 2 * orders, wide), bf16),
            pltpu.VMEM((chunks, planes, 2 * orders, wide), f32),
            pltpu.VMEM((chunks, planes, 2 * orders, wide), bf16),
            pltpu.VMEM((chunks, planes - 1, 2 * orders, wide), bf16),
            pltpu.VMEM((chunks, planes - 1, 2 * orders, wide), bf16),
            pltpu.VMEM((chunks, 2, ma_n, own_n, wide), f32),
            pltpu.VMEM((chunks, ma_n - 1, 2, own_n, wide), bf16),
            pltpu.VMEM((chunks, ma_n - 1, 2, own_n, wide), bf16),
            pltpu.VMEM((share // LANES, own_n, LANES), f32),
            pltpu.VMEM((2 * beam.shape[0], LANES), f32),
            pltpu.VMEM((1, share), f32),
            pltpu.VMEM((ma_n - 1, 1, share), f32),
            dma((3,)),
            dma,
            dma((pieces,)),
            dma,
            dma((2, chunks)),
            dma((2, chunks, planes - 1)),
            dma((2, chunks, ma_n - 1)),
            dma((2, ma_n - 1)),
        ],
        compiler_params=pltpu.CompilerParams(
            collective_id=0, has_side_effects=True, vmem_limit_bytes=56 * 1024 * 1024
        ),
    )(sky_map, legendre, m_list, block_start, beam)
    harm, spec = pl.pallas_call(
        hand_on,
        out_shape=(jax.ShapeDtypeStruct(harm.shape, f32), jax.ShapeDtypeStruct(spec.shape, f32)),
        in_specs=[vmem] * 2,
        out_specs=(vmem, vmem),
    )(harm, spec)
    return harm, spec.reshape(share)


def solution(mesh):
    placed = (P(None, ("blk", "ma"), None), P(("blk", "ma"), None, None), P(), P(), P())
    return jax.shard_map(
        functools.partial(per_device, mesh.shape["blk"], mesh.shape["ma"]),
        mesh=mesh,
        in_specs=placed,
        out_specs=(P(None, "ma", "blk"), P("blk")),
        check_vma=False,
    )
```
